512 devices in a mesh: row: 16 (over x_hi, z), col: 32 (over y, x_lo, core).
Axes of the slice: x: 4 (x_hi: 2, x_lo: 2; x = x_hi * 2 + x_lo), y: 8, z: 8, core: 2. Of those that a mesh axis runs over, the one named last changes fastest.
Arguments:
- emb: float32 [32768, 128], P(('row', 'col')), may hold values from -1.8 to 1.8
- bias: float32 [32768], P(('row', 'col')), may hold values from -4 to 4
- emb_sq: float32 [32768, 128], P(('row', 'col')), may hold values from 10 to 1000
- bias_sq: float32 [32768], P(('row', 'col')), may hold values from 30000 to 3000000
- tile_rows: int32 [2048], P(('row', 'col')), may hold values from 0 to 15
- tile_cols: int32 [2048], P(('row', 'col')), may hold values from 0 to 7
- tile_live: int32 [512], P(('row', 'col')), may hold values from 1 to 4, 1024 in all
- counts: int32 [2048, 128, 128], P(('row', 'col')), may hold values from 0 to 1023
Outputs:
- emb_out: float32 [32768, 128], P(('row', 'col'))
- bias_out: float32 [32768], P(('row', 'col'))
The draws below stay inside these ranges and needn't reach their ends.
Inputs may be any that keep to these rules, and one draw needn't show every extreme that they name: Each device uses its first tile_live slots and ignores the others; some device uses all 4.
All inputs are finite; a program needn't handle non-finite values.
Results may differ from the reference program's by a relative error of at most 0.005.
Values may be sent and summed in bfloat16 or wider, within the bound.
A program may use at most 64 MiB of HBM per device.

```python
import math
import jax
import jax.numpy as jnp
import numpy as np
from jax import lax

D = 128
TILE = 128
CL_DEV = 64
NT_DEV = 4
STEPS = 2
NCL = 32768
SLOTS = 2048
RB = 2048
CB = 1024
N_ROW = 16
N_COL = 32
DEVICES = 512


def draw_counts(key, part):
    first, second, third = jax.random.split(jax.random.fold_in(key, 7), 3)
    shape = (SLOTS, TILE, TILE)
    exponent = jax.random.randint(first, shape, 0, 10)
    base_value = jnp.left_shift(jnp.ones(shape, jnp.int32), exponent)
    extra = jax.random.randint(second, shape, jnp.zeros(shape, jnp.int32), base_value)
    present = jax.random.randint(third, shape, 0, 2)
    return ((base_value + extra) * present).astype(jnp.int32)


def touch_ends(values, key, low, largest):
    dims = values.shape
    index_at = [jax.random.randint(jax.random.fold_in(key, axis), (), 0, dims[axis]) for axis in range(len(dims))]
    values = values.at[tuple(index_at)].set(low)
    longest = dims.index(max(dims))
    index_at[longest] = (index_at[longest] + 1) % dims[longest]
    return values.at[tuple(index_at)].set(largest)


def shard_levels(key, extent, cuts, least, largest):
    factor_of = 1.0
    for dim, shards_of in cuts:
        heights = jax.random.uniform(jax.random.fold_in(jax.random.fold_in(key, 6), dim), (shards_of,), jnp.float32, least / len(cuts), largest / len(cuts))
        factor_of = factor_of * jnp.repeat(jnp.exp(heights), extent[dim] // shards_of).reshape((-1,) + (1,) * (len(extent) - 1 - dim))
    return factor_of


def rank_bounds(count, lean):
    portions = [(1 << 20) // math.isqrt(grade ** lean) + 1 for grade in range(1, count + 1)]
    scale = 1 + sum(portions) // (1 << 30)
    return np.cumsum(np.array([max(1, weight // scale) for weight in portions]))


def ranked_ids(stream_key, dims, number_of, slope):
    grid = rank_bounds(number_of, slope)
    pick = jax.random.randint(jax.random.fold_in(stream_key, 1), dims, 0, int(grid[number_of - 1]))
    grade = jnp.searchsorted(jnp.asarray(grid, jnp.int32), pick, side="right")
    return jax.random.permutation(jax.random.fold_in(stream_key, 2), number_of)[grade].astype(jnp.int32)


def split_up(count, total, reach, skew):
    loads = [(1 << 20) // math.isqrt(grade ** skew) + 1 for grade in range(2, count + 1)]
    surplus, given = total - reach - (count - 1), [1] * (count - 1)
    while surplus > 0:
        candidates = [i for i in range(count - 1) if given[i] < reach]
        mass, remaining = sum([loads[i] for i in candidates]), surplus
        for i in candidates:
            more = min(reach - given[i], max(1, remaining * loads[i] // mass), surplus)
            given[i] = given[i] + more
            surplus = surplus - more
    return np.array([reach] + given)


def ragged(own_key, number_of, total, limit, slope):
    if number_of == 2:
        one = jax.random.randint(own_key, (), max(1, total - limit), min(limit, total - 1) + 1)
        return jnp.stack([one, total - one])
    sizes = jnp.asarray(split_up(number_of, total, limit, slope), jnp.int32)
    pairs = (number_of - 1) // 2
    giver, sink = sizes[1:1 + 2 * pairs:2], sizes[2:2 + 2 * pairs:2]
    margin = jnp.minimum(giver - 1, limit - sink)
    shifted = jax.random.randint(jax.random.fold_in(own_key, 1), (pairs,), 0, 1 << 20) % (margin + 1)
    sizes = sizes.at[1:1 + 2 * pairs:2].set(giver - shifted).at[2:2 + 2 * pairs:2].set(sink + shifted)
    return sizes[jax.random.permutation(jax.random.fold_in(own_key, 2), number_of)]


def bell_draw(key, shape, width, bound, cuts=(), kind=jnp.bfloat16):
    level = shard_levels(key, shape, cuts, -0.22, 0.18) if cuts else 1.0
    result = jax.random.normal(key, shape, jnp.float32) * width * level
    return jnp.minimum(jnp.maximum(result, -bound), bound).astype(kind)


def setup_inputs(seed: int = 0) -> dict:
    streams_of = jax.random.split(jax.random.key(seed), 9)
    emb = bell_draw(streams_of[0], (NCL, D), 0.3, 1.8, ((0, 512),), jnp.float32)
    bias = bell_draw(streams_of[1], (NCL,), 1.0, 4.0, ((0, 512),), jnp.float32)
    emb_sq = jnp.clip(jnp.exp(math.log(1000.0) - 4.6051702 * jax.random.uniform(streams_of[2], (NCL, D), jnp.float32) ** shard_levels(streams_of[2], (NCL, D), ((0, 512),), -0.2, 0.2)), 10.0, 1000.0)
    bias_sq = jnp.clip(jnp.exp(math.log(3000000) - 4.6051702 * jax.random.uniform(streams_of[3], (NCL,), jnp.float32) ** shard_levels(streams_of[3], (NCL,), ((0, 512),), -0.2, 0.2)), 30000.0, 3000000)
    tile_rows = touch_ends(ranked_ids(streams_of[4], (SLOTS,), RB // TILE, 2), jax.random.fold_in(streams_of[4], 3), 0, (RB // TILE) - 1).astype(jnp.int32)
    tile_cols = touch_ends(jax.random.randint(streams_of[5], (SLOTS,), 0, CB // TILE), jax.random.fold_in(streams_of[5], 1), 0, (CB // TILE) - 1).astype(jnp.int32)
    tile_live = ragged(streams_of[6], DEVICES, DEVICES * NT_DEV // 2, NT_DEV, 2).astype(jnp.int32)
    counts = draw_counts(jax.random.fold_in(streams_of[8], 71), 0)
    return dict(emb=emb, bias=bias, emb_sq=emb_sq, bias_sq=bias_sq, tile_rows=tile_rows, tile_cols=tile_cols, tile_live=tile_live, counts=counts)


learn_rate = 0.1
count_cap = 100.0

def pair_weights(counts):
    amounts = counts.astype(jnp.float32)
    weight = jnp.minimum(1.0, jnp.power(amounts / count_cap, 0.75))
    target = jnp.log(jnp.maximum(amounts, 1.0))
    return (weight, target)

def device_terms(rows_half, rows_bias, cols_half, cols_bias, rows_index, cols_index, live_count, weight, target):
    left_tiles = rows_half.reshape(RB // TILE, TILE, D)[rows_index].astype(jnp.float32)
    right_tiles = cols_half.reshape(CB // TILE, TILE, D)[cols_index].astype(jnp.float32)
    left_bias = rows_bias.reshape(RB // TILE, TILE)[rows_index].astype(jnp.float32)
    right_bias = cols_bias.reshape(CB // TILE, TILE)[cols_index].astype(jnp.float32)
    scores = jnp.einsum('spd,sqd->spq', left_tiles, right_tiles)
    errors = scores + left_bias[:, :, None] + right_bias[:, None, :] - target
    live_mask = jnp.arange(NT_DEV) < live_count
    residual = jnp.where(live_mask[:, None, None], weight * errors, 0.0)
    resid_half = lax.optimization_barrier(residual.astype(jnp.bfloat16)).astype(jnp.float32)
    grad_left = jnp.einsum('spq,sqd->spd', resid_half, right_tiles)
    grad_right = jnp.einsum('spq,spd->sqd', resid_half, left_tiles)
    row_part = jax.ops.segment_sum(grad_left, rows_index, num_segments=RB // TILE).reshape(RB, D)
    row_bpart = jax.ops.segment_sum(lax.optimization_barrier(jnp.sum(residual, axis=2)), rows_index, num_segments=RB // TILE).reshape(RB)
    col_part = jax.ops.segment_sum(grad_right, cols_index, num_segments=CB // TILE).reshape(CB, D)
    col_bpart = jax.ops.segment_sum(lax.optimization_barrier(jnp.sum(residual, axis=1)), cols_index, num_segments=CB // TILE).reshape(CB)
    return (row_part, row_bpart, col_part, col_bpart)

def adagrad_step(values, accum, grads):
    new_accum = accum + grads * grads
    return (values - learn_rate * grads / jnp.sqrt(new_accum), new_accum)

def reference(emb, bias, emb_sq, bias_sq, tile_rows, tile_cols, tile_live, counts):
    values, bias_values, accum, bias_accum = (emb, bias, emb_sq, bias_sq)
    devices = jnp.arange(N_ROW * N_COL, dtype=jnp.int32)
    for step_index in range(STEPS):
        emb_grid = values.astype(jnp.bfloat16).reshape(N_ROW, N_COL, CL_DEV, D)
        bias_grid = bias_values.astype(jnp.bfloat16).reshape(N_ROW, N_COL, CL_DEV)

        def visit(carry, device):
            grad_sum, bias_sum = carry
            row_rank = device // N_COL
            col_rank = device % N_COL
            rows_half = lax.dynamic_index_in_dim(emb_grid, row_rank, 0, keepdims=False).reshape(RB, D)
            rows_bias = lax.dynamic_index_in_dim(bias_grid, row_rank, 0, keepdims=False).reshape(RB)
            cols_half = lax.dynamic_index_in_dim(emb_grid, col_rank, 1, keepdims=False).reshape(CB, D)
            cols_bias = lax.dynamic_index_in_dim(bias_grid, col_rank, 1, keepdims=False).reshape(CB)
            offset = device * NT_DEV
            rows_index = lax.dynamic_slice_in_dim(tile_rows, offset, NT_DEV)
            cols_index = lax.dynamic_slice_in_dim(tile_cols, offset, NT_DEV)
            tiles = lax.dynamic_slice_in_dim(counts, offset, NT_DEV, 0)
            weight, target = pair_weights(tiles)
            live_count = lax.dynamic_index_in_dim(tile_live, device, 0, keepdims=False)
            row_part, row_bpart, col_part, col_bpart = device_terms(rows_half, rows_bias, cols_half, cols_bias, rows_index, cols_index, live_count, weight, target)
            by_rows = grad_sum.reshape(N_ROW, RB, D)
            segment = lax.dynamic_index_in_dim(by_rows, row_rank, 0, keepdims=False) + row_part
            by_rows = lax.dynamic_update_index_in_dim(by_rows, segment, row_rank, 0)
            by_cells = by_rows.reshape(N_ROW, N_COL, CL_DEV, D)
            column = lax.dynamic_index_in_dim(by_cells, col_rank, 1, keepdims=False) + col_part.reshape(N_ROW, CL_DEV, D)
            by_cells = lax.dynamic_update_index_in_dim(by_cells, column, col_rank, 1)
            brows = bias_sum.reshape(N_ROW, RB)
            bsegment = lax.dynamic_index_in_dim(brows, row_rank, 0, keepdims=False) + row_bpart
            brows = lax.dynamic_update_index_in_dim(brows, bsegment, row_rank, 0)
            bcells = brows.reshape(N_ROW, N_COL, CL_DEV)
            bcolumn = lax.dynamic_index_in_dim(bcells, col_rank, 1, keepdims=False) + col_bpart.reshape(N_ROW, CL_DEV)
            bcells = lax.dynamic_update_index_in_dim(bcells, bcolumn, col_rank, 1)
            return ((by_cells.reshape(NCL, D), bcells.reshape(NCL)), None)
        start = (jnp.zeros((NCL, D), jnp.float32), jnp.zeros((NCL,), jnp.float32))
        (grad_sum, bias_sum), _ = lax.scan(visit, start, devices)
        values, accum = adagrad_step(values, accum, grad_sum)
        bias_values, bias_accum = adagrad_step(bias_values, bias_accum, bias_sum)
    return (values, bias_values)
```

```python
import functools

import jax
import jax.numpy as jnp
from jax import lax
from jax.experimental import pallas as pl
from jax.experimental.pallas import tpu as pltpu
from jax.sharding import PartitionSpec as P

MESH = pl.DeviceIdType.MESH
D = 128
TILE = 128
HALF = 64
NT = 4
STEPS = 2
RW = 80
ROW_TILES = 16
COL_TILES = 8
NEAR = 15

learn_rate = 0.1
count_cap = 100.0

F32 = jnp.float32
BF16 = jnp.bfloat16


ROW_OFF = sorted(
    [(a, b) for a in range(8) for b in range(2) if a or b], key=lambda o: -(min(o[0], 8 - o[0]) + o[1])
)
COL_OFF = sorted(
    [(a, b) for a in range(8) for b in range(2) if a or b], key=lambda o: -(min(o[0], 8 - o[0]) + 2 * o[1])
)


def dot(a, b, dims):
    return lax.dot_general(a, b, (dims, ((), ())), preferred_element_type=F32)


def body(
    emb_hbm, bias_hbm, esq_hbm, bsq_hbm, counts_hbm, trow, tcol, tlive,
    emb_out, bias_out,
    vals, bvals, acc, bacc, cnt, weight, target,
    msg, rowbuf, colbuf, gleft, gright, gbias, xsend, xrecv, rsend, rrecv, csend, crecv,
    in_sem, ag_ss, ag_rs, fw_ss, fw_rs, rs_ss, rs_rs,
):
    r, c = lax.axis_index("row"), lax.axis_index("col")
    xh, z = r // 8, r % 8
    y, xl, co = c // 4, (c // 2) % 2, c % 2
    chip = c // 2

    def row_chip(off):
        return ((y + off[0]) % 8) * 2 + (xl + off[1]) % 2

    def col_rank(off):
        return ((xh + off[1]) % 2) * 8 + (z + off[0]) % 8

    def row_src(off):
        return ((y + 8 - off[0]) % 8) * 2 + (xl + 2 - off[1]) % 2

    def col_src(off):
        return ((xh + 2 - off[1]) % 2) * 8 + (z + 8 - off[0]) % 8

    other = (r, chip * 2 + 1 - co)

    loads = [
        pltpu.make_async_copy(emb_hbm, vals, in_sem.at[0]),
        pltpu.make_async_copy(esq_hbm, acc, in_sem.at[1]),
        pltpu.make_async_copy(counts_hbm, cnt, in_sem.at[2]),
        pltpu.make_async_copy(bias_hbm, bvals, in_sem.at[3]),
        pltpu.make_async_copy(bsq_hbm, bacc, in_sem.at[4]),
    ]
    for load in loads:
        load.start()

    barrier = pltpu.get_barrier_semaphore()
    for off in ROW_OFF:
        pl.semaphore_signal(barrier, inc=1, device_id=(r, row_chip(off) * 2 + co), device_id_type=MESH)
    for off in COL_OFF:
        pl.semaphore_signal(barrier, inc=1, device_id=(col_rank(off), c), device_id_type=MESH)
    pl.semaphore_signal(barrier, inc=1, device_id=other, device_id_type=MESH)

    loads[0].wait()
    loads[1].wait()
    loads[3].wait()
    loads[4].wait()
    live = tlive[0]
    gleft[NT] = jnp.zeros((2, HALF, D), BF16)
    gright[NT] = jnp.zeros((2, HALF, D), BF16)
    gbias[NT] = jnp.zeros((2, 16, D), BF16)
    low_lanes = lax.broadcasted_iota(jnp.int32, (16, D), 1) < HALF
    first_row = lax.broadcasted_iota(jnp.int32, (16, D), 0)
    one_rows = jnp.ones((16, D), BF16)

    pl.semaphore_wait(barrier, 2 * NEAR + 1)

    for step in range(STEPS):
        sends = []
        msg[step, 0:HALF] = vals[...].astype(BF16)
        msg[step, HALF:RW] = jnp.broadcast_to(bvals[...], (RW - HALF, D)).astype(BF16)
        row_copies, col_copies = [], []
        for k, off in enumerate(ROW_OFF):
            row_copies.append(
                pltpu.make_async_remote_copy(
                    src_ref=msg.at[step], dst_ref=rowbuf.at[step, c],
                    send_sem=ag_ss.at[step, k], recv_sem=ag_rs.at[step, k],
                    device_id=(r, row_chip(off) * 2 + co), device_id_type=MESH,
                )
            )
        for k, off in enumerate(COL_OFF):
            col_copies.append(
                pltpu.make_async_remote_copy(
                    src_ref=msg.at[step], dst_ref=colbuf.at[step, r],
                    send_sem=ag_ss.at[step, NEAR + k], recv_sem=ag_rs.at[step, NEAR + k],
                    device_id=(col_rank(off), c), device_id_type=MESH,
                )
            )
        for a, b in zip(row_copies, col_copies):
            a.start()
            b.start()
        own = pltpu.make_async_remote_copy(
            src_ref=msg.at[step], dst_ref=rowbuf.at[step, c],
            send_sem=fw_ss.at[step, NEAR], recv_sem=fw_rs.at[step, NEAR],
            device_id=other, device_id_type=MESH,
        )
        own.start()
        sends += row_copies + col_copies + [own]
        rowbuf[step, c] = msg[step]
        colbuf[step, r] = msg[step]

        if step == 0:
            loads[2].wait()
            for s in range(NT):
                amounts = cnt[s].astype(F32)
                share = amounts / count_cap
                root = jnp.sqrt(share)
                w = jnp.minimum(1.0, root * jnp.sqrt(root))
                weight[s] = jnp.where(s < live, w, 0.0)
                target[s] = jnp.log(jnp.maximum(amounts, 1.0))

        forwards = []
        for k in reversed(range(NEAR)):
            row_copies[k].wait_recv()
            slot = row_src(ROW_OFF[k]) * 2 + co
            forward = pltpu.make_async_remote_copy(
                src_ref=rowbuf.at[step, slot], dst_ref=rowbuf.at[step, slot],
                send_sem=fw_ss.at[step, k], recv_sem=fw_rs.at[step, k],
                device_id=other, device_id_type=MESH,
            )
            forward.start()
            forwards.append(forward)
        sends += forwards
        for copy in col_copies:
            copy.wait_recv()
        own.wait_recv()
        for forward in forwards:
            forward.wait_recv()

        lefts, rights = [], []
        for s in range(NT):
            ti, tj = trow[s], tcol[s]
            e_i = rowbuf[step, pl.ds(2 * ti, 2), 0:HALF, :].reshape(TILE, D)
            e_j = colbuf[step, pl.ds(2 * tj, 2), 0:HALF, :].reshape(TILE, D)
            b_i = jnp.where(low_lanes, rowbuf[step, 2 * ti, HALF:RW, :], rowbuf[step, 2 * ti + 1, HALF:RW, :])
            b_j = jnp.where(low_lanes, colbuf[step, 2 * tj, HALF:RW, :], colbuf[step, 2 * tj + 1, HALF:RW, :])
            zero = jnp.zeros((16, D), BF16)
            one = jnp.ones((16, D), BF16)
            lhs = jnp.where(first_row == 0, b_i, jnp.where(first_row == 1, one, zero))
            rhs = jnp.where(first_row == 0, one, jnp.where(first_row == 1, b_j, zero))
            score = dot(e_i, e_j, ((1,), (1,))) + dot(lhs, rhs, ((0,), (0,)))
            resid = (weight[s] * (score - target[s])).astype(BF16)
            lefts.append((dot(resid, e_j, ((1,), (0,))), dot(one_rows, resid, ((1,), (1,)))))
            rights.append((dot(resid, e_i, ((0,), (0,))), dot(one_rows, resid, ((1,), (0,)))))

        for store, side, terms, ids in ((gleft, 0, lefts, trow), (gright, 1, rights, tcol)):
            for s in range(NT):
                total, btotal = terms[s]
                for o in range(NT):
                    if o != s:
                        same = jnp.where(ids[o] == ids[s], 1.0, 0.0)
                        total = total + same * terms[o][0]
                        btotal = btotal + same * terms[o][1]
                store[s] = total.astype(BF16).reshape(2, HALF, D)
                gbias[s, side] = btotal.astype(BF16)

        def slot_of(ids, tile):
            found = jnp.int32(NT)
            for s in range(NT):
                found = jnp.where(ids[s] == tile, s, found)
            return found

        row_slots = [slot_of(trow, t) for t in range(ROW_TILES)]
        for t in range(ROW_TILES):
            xsend[step, t, 0:HALF] = gleft[row_slots[t], 1 - co]
            xsend[step, t, HALF:RW] = gbias[row_slots[t], 0]
        cross = pltpu.make_async_remote_copy(
            src_ref=xsend.at[step], dst_ref=xrecv.at[step],
            send_sem=rs_ss.at[step, 2 * NEAR], recv_sem=rs_rs.at[step, 2 * NEAR],
            device_id=other, device_id_type=MESH,
        )
        cross.start()
        sends.append(cross)
        for t in range(COL_TILES):
            slot = slot_of(tcol, t)
            for h in range(2):
                csend[step, 2 * t + h, 0:HALF] = gright[slot, h]
                csend[step, 2 * t + h, HALF:RW] = gbias[slot, 1]
        col_copies = []
        for k, off in enumerate(COL_OFF):
            copy = pltpu.make_async_remote_copy(
                src_ref=csend.at[step, col_rank(off)], dst_ref=crecv.at[step, k],
                send_sem=rs_ss.at[step, NEAR + k], recv_sem=rs_rs.at[step, NEAR + k],
                device_id=(col_rank(off), c), device_id_type=MESH,
            )
            copy.start()
            col_copies.append(copy)
        sends += col_copies
        cross.wait_recv()
        for t in range(ROW_TILES):
            rsend[step, t, 0:HALF] = (
                gleft[row_slots[t], co].astype(F32) + xrecv[step, t, 0:HALF].astype(F32)
            ).astype(BF16)
            rsend[step, t, HALF:RW] = (
                gbias[row_slots[t], 0].astype(F32) + xrecv[step, t, HALF:RW].astype(F32)
            ).astype(BF16)
        row_copies = []
        for k, off in enumerate(ROW_OFF):
            copy = pltpu.make_async_remote_copy(
                src_ref=rsend.at[step, row_chip(off)], dst_ref=rrecv.at[step, k],
                send_sem=rs_ss.at[step, k], recv_sem=rs_rs.at[step, k],
                device_id=(r, row_chip(off) * 2 + co), device_id_type=MESH,
            )
            copy.start()
            row_copies.append(copy)
        sends += row_copies

        grad = rsend[step, chip].astype(F32)
        cgrad = csend[step, r].astype(F32)
        for k in reversed(range(NEAR)):
            col_copies[k].wait_recv()
            cgrad = cgrad + crecv[step, k].astype(F32)
        for k in reversed(range(NEAR)):
            row_copies[k].wait_recv()
            grad = grad + rrecv[step, k].astype(F32)

        g = grad[0:HALF] + cgrad[0:HALF]
        new_acc = acc[...] + g * g
        new_vals = vals[...] - learn_rate * g / jnp.sqrt(new_acc)
        lane_half = lax.broadcasted_iota(jnp.int32, (8, D), 1) // HALF
        row_b = jnp.where(lane_half == co, grad[HALF:HALF + 8], 0.0)
        col_b = jnp.where(lane_half == z % 2, cgrad[HALF:HALF + 8], 0.0)
        bg = row_b + pltpu.roll(row_b, HALF, 1) + col_b + pltpu.roll(col_b, HALF, 1)
        bg = bg[0:1]
        new_bacc = bacc[...] + bg * bg
        new_bvals = bvals[...] - learn_rate * bg / jnp.sqrt(new_bacc)
        if step + 1 < STEPS:
            vals[...] = new_vals
            acc[...] = new_acc
            bvals[...] = new_bvals
            bacc[...] = new_bacc
        else:
            emb_out[...] = new_vals
            bias_out[...] = new_bvals
        for copy in sends:
            copy.wait_send()


def per_device(emb, bias, emb_sq, bias_sq, tile_rows, tile_cols, tile_live, counts):
    twice = lambda v: jnp.concatenate([v, v]).reshape(1, D)
    any_spec = pl.BlockSpec(memory_space=pl.ANY)
    smem = pl.BlockSpec(memory_space=pltpu.SMEM)
    vmem = pl.BlockSpec(memory_space=pltpu.VMEM)
    emb_out, bias_out = pl.pallas_call(
        body,
        out_shape=(jax.ShapeDtypeStruct((HALF, D), F32), jax.ShapeDtypeStruct((1, D), F32)),
        in_specs=[any_spec] * 5 + [smem] * 3,
        out_specs=(vmem, vmem),
        scratch_shapes=[
            pltpu.VMEM((HALF, D), F32),
            pltpu.VMEM((1, D), F32),
            pltpu.VMEM((HALF, D), F32),
            pltpu.VMEM((1, D), F32),
            pltpu.VMEM((NT, TILE, TILE), jnp.int32),
            pltpu.VMEM((NT, TILE, TILE), F32),
            pltpu.VMEM((NT, TILE, TILE), F32),
            pltpu.VMEM((STEPS, RW, D), BF16),
            pltpu.VMEM((STEPS, 2 * ROW_TILES, RW, D), BF16),
            pltpu.VMEM((STEPS, 2 * COL_TILES, RW, D), BF16),
            pltpu.VMEM((NT + 1, 2, HALF, D), BF16),
            pltpu.VMEM((NT + 1, 2, HALF, D), BF16),
            pltpu.VMEM((NT + 1, 2, 16, D), BF16),
            pltpu.VMEM((STEPS, ROW_TILES, RW, D), BF16),
            pltpu.VMEM((STEPS, ROW_TILES, RW, D), BF16),
            pltpu.VMEM((STEPS, ROW_TILES, RW, D), BF16),
            pltpu.VMEM((STEPS, NEAR, RW, D), BF16),
            pltpu.VMEM((STEPS, 2 * COL_TILES, RW, D), BF16),
            pltpu.VMEM((STEPS, NEAR, RW, D), BF16),
            pltpu.SemaphoreType.DMA((5,)),
            pltpu.SemaphoreType.DMA((STEPS, 2 * NEAR)),
            pltpu.SemaphoreType.DMA((STEPS, 2 * NEAR)),
            pltpu.SemaphoreType.DMA((STEPS, NEAR + 1)),
            pltpu.SemaphoreType.DMA((STEPS, NEAR + 1)),
            pltpu.SemaphoreType.DMA((STEPS, 2 * NEAR + 1)),
            pltpu.SemaphoreType.DMA((STEPS, 2 * NEAR + 1)),
        ],
        compiler_params=pltpu.CompilerParams(
            collective_id=0, has_side_effects=True, vmem_limit_bytes=40 * 1024 * 1024
        ),
    )(emb, twice(bias), emb_sq, twice(bias_sq), counts, tile_rows, tile_cols, tile_live)
    return (emb_out, bias_out[0, :HALF])


def solution(mesh):
    placed = (
        P(("row", "col"), None),
        P(("row", "col")),
        P(("row", "col"), None),
        P(("row", "col")),
        P(("row", "col")),
        P(("row", "col")),
        P(("row", "col")),
        P(("row", "col"), None, None),
    )
    return jax.shard_map(
        per_device,
        mesh=mesh,
        in_specs=placed,
        out_specs=(P(("row", "col"), None), P(("row", "col"))),
        check_vma=False,
    )
```

```python
import jax
import jax.numpy as jnp
from jax import lax
from jax.experimental import pallas as pl
from jax.experimental.pallas import tpu as pltpu
from jax.sharding import PartitionSpec as P

MESH = pl.DeviceIdType.MESH
D = 128
TILE = 128
HALF = 64
NT = 4
STEPS = 2
ROW_TILES = 16
COL_TILES = 8
NEAR = 15
GROUPS = 3
PER = NEAR // GROUPS

learn_rate = 0.1
count_cap = 100.0

F32 = jnp.float32
BF16 = jnp.bfloat16

OFFSETS = [(a, b) for a in range(8) for b in range(2) if a or b]
ROW_OFF = sorted(OFFSETS, key=lambda o: -(min(o[0], 8 - o[0]) + o[1]))
COL_OFF = sorted(OFFSETS, key=lambda o: -(min(o[0], 8 - o[0]) + 2 * o[1]))


def dot(a, b, dims):
    return lax.dot_general(a, b, (dims, ((), ())), preferred_element_type=F32)


def body(
    emb_hbm, bias_hbm, esq_hbm, bsq_hbm, counts_hbm, trow_hbm, tcol_hbm, tlive_hbm,
    emb_out, bias_out,
    vals, bhalf, acc, bsqhalf, bvals, bacc, cnt, weight, target,
    trow, tcol, tlive, orow_in, orow,
    msg, bmsg, rowbuf, rowb, colbuf, colb, xsend, xbsend, xrecv, xbrecv,
    gown, goth, gbias, gright, cbias, hrecv, hbrecv,
    rsend, rbsend, rrecv, rbrecv, csend, cbsend, crecv, cbrecv,
    in_sem, id_ss, id_rs, ag_ss, ag_rs, x_ss, x_rs, rs_ss, rs_rs, rsb_ss, rsb_rs,
):
    r, c = lax.axis_index("row"), lax.axis_index("col")
    xh, z = r // 8, r % 8
    y, xl, co = c // 4, (c // 2) % 2, c % 2
    chip = c // 2

    def row_chip(off):
        return ((y + off[0]) % 8) * 2 + (xl + off[1]) % 2

    def col_rank(off):
        return ((xh + off[1]) % 2) * 8 + (z + off[0]) % 8

    other = (r, chip * 2 + 1 - co)

    def remote(src, dst, ss, rs, device):
        return pltpu.make_async_remote_copy(
            src_ref=src, dst_ref=dst, send_sem=ss, recv_sem=rs, device_id=device, device_id_type=MESH
        )

    def wait_bytes(ref, sem):
        pltpu.make_async_copy(ref, ref, sem).wait()

    loads = [
        pltpu.make_async_copy(src, dst, in_sem.at[i])
        for i, (src, dst) in enumerate(
            (
                (emb_hbm, vals), (bias_hbm, bhalf), (esq_hbm, acc), (bsq_hbm, bsqhalf),
                (counts_hbm, cnt), (trow_hbm, trow), (tcol_hbm, tcol), (tlive_hbm, tlive),
            )
        )
    ]
    for load in loads:
        load.start()

    barrier = pltpu.get_barrier_semaphore()
    for row_off, col_off in zip(ROW_OFF, COL_OFF):
        pl.semaphore_signal(barrier, inc=1, device_id=(col_rank(col_off), c), device_id_type=MESH)
        pl.semaphore_signal(barrier, inc=1, device_id=(r, row_chip(row_off) * 2 + co), device_id_type=MESH)
    pl.semaphore_signal(barrier, inc=1, device_id=other, device_id_type=MESH)

    for load in loads[:4] + loads[5:]:
        load.wait()
    live = tlive[0]
    for store in (gown, hrecv):
        store[NT] = jnp.zeros((HALF, D), BF16)
    gright[NT] = jnp.zeros((2, HALF, D), BF16)
    for store in (gbias, cbias, hbrecv):
        store[NT] = jnp.zeros((1, D), F32)
    bvals[...] = jnp.concatenate([bhalf[...], bhalf[...]], axis=1)
    bacc[...] = jnp.concatenate([bsqhalf[...], bsqhalf[...]], axis=1)
    low = lax.broadcasted_iota(jnp.int32, (1, D), 1) < HALF
    first_row = lax.broadcasted_iota(jnp.int32, (16, D), 0)
    one_rows = jnp.ones((16, D), BF16)

    pl.semaphore_wait(barrier, 2 * NEAR + 1)

    ids = remote(trow_hbm, orow_in, id_ss, id_rs, other)
    for step in range(STEPS):
        half = vals[...].astype(BF16)
        msg[step] = half
        bhalf_now = bvals[...].astype(BF16).astype(F32)
        bmsg[step] = bhalf_now
        for row_off, col_off in zip(ROW_OFF, COL_OFF):
            remote(bmsg.at[step], rowb.at[step, chip], ag_ss.at[step, 0], ag_rs.at[step, 0],
                   (r, row_chip(row_off) * 2 + co)).start()
            remote(bmsg.at[step], colb.at[step, r], ag_ss.at[step, 1], ag_rs.at[step, 1],
                   (col_rank(col_off), c)).start()
        for row_off, col_off in zip(ROW_OFF, COL_OFF):
            remote(msg.at[step], rowbuf.at[step, chip], ag_ss.at[step, 2], ag_rs.at[step, 2],
                   (r, row_chip(row_off) * 2 + co)).start()
            remote(msg.at[step], colbuf.at[step, r], ag_ss.at[step, 3], ag_rs.at[step, 3],
                   (col_rank(col_off), c)).start()
        rowbuf[step, chip] = half
        colbuf[step, r] = half
        rowb[step, chip] = bhalf_now
        colb[step, r] = bhalf_now

        if step == 0:
            ids.start()
            loads[4].wait()
            for s in range(NT):
                for h in range(2):
                    start = pl.multiple_of((co if h == 0 else 1 - co) * HALF, HALF)
                    amounts = cnt[s, pl.ds(start, HALF), :].astype(F32)
                    share = amounts / count_cap
                    root = jnp.sqrt(share)
                    w = jnp.minimum(1.0, root * jnp.sqrt(root))
                    weight[s, h * HALF:(h + 1) * HALF] = jnp.where(s < live, w, 0.0)
                    target[s, h * HALF:(h + 1) * HALF] = jnp.log(jnp.maximum(amounts, 1.0))
            ids.wait_recv()
            fetch = pltpu.make_async_copy(orow_in, orow, in_sem.at[8])
            fetch.start()
            fetch.wait()

        wait_bytes(rowb.at[step, pl.ds(0, NEAR)], ag_rs.at[step, 0])
        wait_bytes(rowbuf.at[step, pl.ds(0, NEAR)], ag_rs.at[step, 2])
        for s in range(NT):
            xsend[step, s] = rowbuf[step, orow[s]]
            xbsend[step, s] = rowb[step, orow[s]]
        cross = remote(xsend.at[step], xrecv.at[step], x_ss.at[step, 0], x_rs.at[step, 0], other)
        bcross = remote(xbsend.at[step], xbrecv.at[step], x_ss.at[step, 1], x_rs.at[step, 1], other)
        cross.start()
        bcross.start()
        wait_bytes(colb.at[step, pl.ds(0, NEAR)], ag_rs.at[step, 1])
        wait_bytes(colbuf.at[step, pl.ds(0, NEAR)], ag_rs.at[step, 3])
        cross.wait_recv()
        bcross.wait_recv()

        e_is, resids, lefts = [], [], []
        for s in range(NT):
            ti, tj = trow[s], tcol[s]
            e_i = jnp.concatenate([rowbuf[step, ti], xrecv[step, s]], axis=0)
            e_j = colbuf[step, pl.ds(2 * tj, 2)].reshape(TILE, D)
            b_i = jnp.where(low, rowb[step, ti], xbrecv[step, s])
            b_j = jnp.where(low, colb[step, 2 * tj], colb[step, 2 * tj + 1])
            lhs = jnp.where(first_row == 0, b_i, jnp.where(first_row == 1, 1.0, 0.0)).astype(BF16)
            rhs = jnp.where(first_row == 0, 1.0, jnp.where(first_row == 1, b_j, 0.0)).astype(BF16)
            score = dot(e_i, e_j, ((1,), (1,))) + dot(lhs, rhs, ((0,), (0,)))
            resid = (weight[s] * (score - target[s])).astype(BF16)
            e_is.append(e_i)
            resids.append(resid)
            lefts.append((dot(resid, e_j, ((1,), (0,))), dot(one_rows, resid, ((1,), (1,)))[0:1]))

        def merged(terms, ids):
            for s in range(NT):
                total, btotal = terms[s]
                for o in range(NT):
                    if o != s:
                        same = jnp.where(ids[o] == ids[s], 1.0, 0.0)
                        total = total + same * terms[o][0]
                        btotal = btotal + same * terms[o][1]
                yield s, total.astype(BF16), btotal

        for s, total, btotal in merged(lefts, trow):
            gown[s] = total[0:HALF]
            goth[step, s] = total[HALF:TILE]
            gbias[s] = btotal
        hcross = remote(goth.at[step], hrecv.at[pl.ds(0, NT)], x_ss.at[step, 2], x_rs.at[step, 2], other)
        hbcross = remote(gbias.at[pl.ds(0, NT)], hbrecv.at[pl.ds(0, NT)], x_ss.at[step, 3], x_rs.at[step, 3], other)
        hcross.start()
        hbcross.start()

        rights = [
            (dot(resids[s], e_is[s], ((0,), (0,))), dot(one_rows, resids[s], ((1,), (0,)))[0:1]) for s in range(NT)
        ]
        for s, total, btotal in merged(rights, tcol):
            gright[s] = total.reshape(2, HALF, D)
            cbias[s] = btotal

        def slot_of(ids, tile):
            found = jnp.int32(NT)
            for s in range(NT):
                found = jnp.where(ids[s] == tile, s, found)
            return found

        for t in range(COL_TILES):
            slot = slot_of(tcol, t)
            csend[step, 2 * t:2 * t + 2] = gright[slot]
            cbsend[step, 2 * t] = cbias[slot]
            cbsend[step, 2 * t + 1] = cbias[slot]
        for k, off in enumerate(COL_OFF):
            to = col_rank(off)
            remote(cbsend.at[step, to], cbrecv.at[step, k], rsb_ss.at[step, 1], rsb_rs.at[step, 1], (to, c)).start()
        for k, off in enumerate(COL_OFF):
            to = col_rank(off)
            remote(csend.at[step, to], crecv.at[step, k], rs_ss.at[step, 1],
                   rs_rs.at[step, 1, k // PER], (to, c)).start()

        hcross.wait_recv()
        hbcross.wait_recv()
        for t in range(ROW_TILES):
            mine, its = slot_of(trow, t), slot_of(orow, t)
            rsend[step, t] = gown[mine] + hrecv[its]
            rbsend[step, t] = gbias[mine] + pltpu.roll(hbrecv[its], HALF, 1)
        for k, off in enumerate(ROW_OFF):
            to = row_chip(off)
            remote(rbsend.at[step, to], rbrecv.at[step, k], rsb_ss.at[step, 0], rsb_rs.at[step, 0],
                   (r, to * 2 + co)).start()
        for k, off in enumerate(ROW_OFF):
            to = row_chip(off)
            remote(rsend.at[step, to], rrecv.at[step, k], rs_ss.at[step, 0],
                   rs_rs.at[step, 0, k // PER], (r, to * 2 + co)).start()

        g = rsend[step, chip].astype(F32) + csend[step, r].astype(F32)
        wait_bytes(cbrecv.at[step], rsb_rs.at[step, 1])
        wait_bytes(rbrecv.at[step], rsb_rs.at[step, 0])
        row_b, col_b = rbsend[step, chip], cbsend[step, r]
        for k in range(NEAR):
            row_b = row_b + rbrecv[step, k]
            col_b = col_b + cbrecv[step, k]
        for half_id, store in ((1, crecv), (0, rrecv)):
            for group in range(GROUPS):
                wait_bytes(store.at[step, pl.ds(group * PER, PER)], rs_rs.at[step, half_id, group])
                for k in range(group * PER, (group + 1) * PER):
                    g = g + store[step, k].astype(F32)

        new_acc = acc[...] + g * g
        new_vals = vals[...] - learn_rate * g / jnp.sqrt(new_acc)
        lane_half = lax.broadcasted_iota(jnp.int32, (1, D), 1) // HALF
        row_b = jnp.where(low, row_b, 0.0)
        col_b = jnp.where(lane_half == z % 2, col_b, 0.0)
        both = row_b + col_b
        bg = both + pltpu.roll(both, HALF, 1)
        new_bacc = bacc[...] + bg * bg
        new_bvals = bvals[...] - learn_rate * bg / jnp.sqrt(new_bacc)
        if step + 1 < STEPS:
            vals[...] = new_vals
            acc[...] = new_acc
            bvals[...] = new_bvals
            bacc[...] = new_bacc
        else:
            emb_out[...] = new_vals
            bias_out[...] = new_bvals[:, 0:HALF]

        if step == 0:
            ids.wait_send()
        for sem, ref in (
            (ag_ss.at[step, 0], rbrecv), (ag_ss.at[step, 1], rbrecv),
            (ag_ss.at[step, 2], rrecv), (ag_ss.at[step, 3], rrecv),
            (rs_ss.at[step, 0], rrecv), (rs_ss.at[step, 1], rrecv),
            (rsb_ss.at[step, 0], rbrecv), (rsb_ss.at[step, 1], rbrecv),
        ):
            wait_bytes(ref.at[step], sem)
        for copy in (cross, bcross, hcross, hbcross):
            copy.wait_send()


def per_device(emb, bias, emb_sq, bias_sq, tile_rows, tile_cols, tile_live, counts):
    hbm = pl.BlockSpec(memory_space=pltpu.HBM)
    vmem = pl.BlockSpec(memory_space=pltpu.VMEM)
    emb_out, bias_out = pl.pallas_call(
        body,
        out_shape=(jax.ShapeDtypeStruct((HALF, D), F32), jax.ShapeDtypeStruct((1, HALF), F32)),
        in_specs=[hbm] * 8,
        out_specs=(vmem, vmem),
        scratch_shapes=[
            pltpu.VMEM((HALF, D), F32),
            pltpu.VMEM((1, HALF), F32),
            pltpu.VMEM((HALF, D), F32),
            pltpu.VMEM((1, HALF), F32),
            pltpu.VMEM((1, D), F32),
            pltpu.VMEM((1, D), F32),
            pltpu.VMEM((NT, TILE, TILE), jnp.int32),
            pltpu.VMEM((NT, TILE, TILE), F32),
            pltpu.VMEM((NT, TILE, TILE), F32),
            pltpu.SMEM((NT,), jnp.int32),
            pltpu.SMEM((NT,), jnp.int32),
            pltpu.SMEM((1,), jnp.int32),
            pltpu.VMEM((NT,), jnp.int32),
            pltpu.SMEM((NT,), jnp.int32),
            pltpu.VMEM((STEPS, HALF, D), BF16),
            pltpu.VMEM((STEPS, 1, D), F32),
            pltpu.VMEM((STEPS, ROW_TILES, HALF, D), BF16),
            pltpu.VMEM((STEPS, ROW_TILES, 1, D), F32),
            pltpu.VMEM((STEPS, 2 * COL_TILES, HALF, D), BF16),
            pltpu.VMEM((STEPS, 2 * COL_TILES, 1, D), F32),
            pltpu.VMEM((STEPS, NT, HALF, D), BF16),
            pltpu.VMEM((STEPS, NT, 1, D), F32),
            pltpu.VMEM((STEPS, NT, HALF, D), BF16),
            pltpu.VMEM((STEPS, NT, 1, D), F32),
            pltpu.VMEM((NT + 1, HALF, D), BF16),
            pltpu.VMEM((STEPS, NT, HALF, D), BF16),
            pltpu.VMEM((NT + 1, 1, D), F32),
            pltpu.VMEM((NT + 1, 2, HALF, D), BF16),
            pltpu.VMEM((NT + 1, 1, D), F32),
            pltpu.VMEM((NT + 1, HALF, D), BF16),
            pltpu.VMEM((NT + 1, 1, D), F32),
            pltpu.VMEM((STEPS, ROW_TILES, HALF, D), BF16),
            pltpu.VMEM((STEPS, ROW_TILES, 1, D), F32),
            pltpu.VMEM((STEPS, NEAR, HALF, D), BF16),
            pltpu.VMEM((STEPS, NEAR, 1, D), F32),
            pltpu.VMEM((STEPS, 2 * COL_TILES, HALF, D), BF16),
            pltpu.VMEM((STEPS, 2 * COL_TILES, 1, D), F32),
            pltpu.VMEM((STEPS, NEAR, HALF, D), BF16),
            pltpu.VMEM((STEPS, NEAR, 1, D), F32),
            pltpu.SemaphoreType.DMA((9,)),
            pltpu.SemaphoreType.DMA,
            pltpu.SemaphoreType.DMA,
            pltpu.SemaphoreType.DMA((STEPS, 4)),
            pltpu.SemaphoreType.DMA((STEPS, 4)),
            pltpu.SemaphoreType.DMA((STEPS, 4)),
            pltpu.SemaphoreType.DMA((STEPS, 4)),
            pltpu.SemaphoreType.DMA((STEPS, 2)),
            pltpu.SemaphoreType.DMA((STEPS, 2, GROUPS)),
            pltpu.SemaphoreType.DMA((STEPS, 2)),
            pltpu.SemaphoreType.DMA((STEPS, 2)),
        ],
        compiler_params=pltpu.CompilerParams(
            collective_id=0, has_side_effects=True, vmem_limit_bytes=56 * 1024 * 1024
        ),
    )(
        emb, bias.reshape(1, HALF), emb_sq, bias_sq.reshape(1, HALF), counts,
        tile_rows, tile_cols, tile_live,
    )
    return (emb_out, bias_out.reshape(HALF))


def solution(mesh):
    placed = (
        P(("row", "col"), None),
        P(("row", "col")),
        P(("row", "col"), None),
        P(("row", "col")),
        P(("row", "col")),
        P(("row", "col")),
        P(("row", "col")),
        P(("row", "col"), None, None),
    )
    return jax.shard_map(
        per_device,
        mesh=mesh,
        in_specs=placed,
        out_specs=(P(("row", "col"), None), P(("row", "col"))),
        check_vma=False,
    )
```

```python
import jax
import jax.numpy as jnp
from jax import lax
from jax.experimental import pallas as pl
from jax.experimental.pallas import tpu as pltpu
from jax.sharding import PartitionSpec as P

MESH = pl.DeviceIdType.MESH
D = 128
TILE = 128
HALF = 64
NT = 4
STEPS = 2
ROW_TILES = 16
COL_TILES = 8
NEAR = 15
GROUPS = 3
PER = NEAR // GROUPS

learn_rate = 0.1
count_cap = 100.0

F32 = jnp.float32
BF16 = jnp.bfloat16

OFFSETS = [(a, b) for a in range(8) for b in range(2) if a or b]
ROW_OFF = sorted(OFFSETS, key=lambda o: -(min(o[0], 8 - o[0]) + o[1]))
COL_OFF = sorted(OFFSETS, key=lambda o: -(min(o[0], 8 - o[0]) + 2 * o[1]))


def dot(a, b, dims):
    return lax.dot_general(a, b, (dims, ((), ())), preferred_element_type=F32)


def body(
    emb_hbm, bias_hbm, esq_hbm, bsq_hbm, counts_hbm, trow_hbm, tcol_hbm, tlive,
    emb_out, bias_out,
    vals, bhalf, acc, bsqhalf, bvals, bacc, cnt, weight, target,
    trow, tcol, orow_in, orow,
    msg, bmsg, rowbuf, rowb, colbuf, colb, xsend, xbsend, xrecv, xbrecv,
    gown, goth, gbias, gright, cbias, hrecv, hbrecv,
    rsend, rbsend, rrecv, rbrecv, csend, cbsend, crecv, cbrecv,
    in_sem, id_ss, id_rs, ag_ss, ag_rs, x_ss, x_rs, rs_ss, rs_rs, rsb_ss, rsb_rs,
):
    r, c = lax.axis_index("row"), lax.axis_index("col")
    xh, z = r // 8, r % 8
    y, xl, co = c // 4, (c // 2) % 2, c % 2
    chip = c // 2

    def row_chip(off):
        return ((y + off[0]) % 8) * 2 + (xl + off[1]) % 2

    def col_rank(off):
        return ((xh + off[1]) % 2) * 8 + (z + off[0]) % 8

    other = (r, chip * 2 + 1 - co)

    def remote(src, dst, ss, rs, device):
        return pltpu.make_async_remote_copy(
            src_ref=src, dst_ref=dst, send_sem=ss, recv_sem=rs, device_id=device, device_id_type=MESH
        )

    def wait_bytes(ref, sem):
        pltpu.make_async_copy(ref, ref, sem).wait()

    loads = [
        pltpu.make_async_copy(src, dst, in_sem.at[i])
        for i, (src, dst) in enumerate(
            (
                (emb_hbm, vals), (bias_hbm, bhalf), (esq_hbm, acc), (bsq_hbm, bsqhalf),
                (counts_hbm, cnt), (trow_hbm, trow), (tcol_hbm, tcol),
            )
        )
    ]
    barrier = pltpu.get_barrier_semaphore()
    for row_off, col_off in zip(ROW_OFF, COL_OFF):
        pl.semaphore_signal(barrier, inc=1, device_id=(col_rank(col_off), c), device_id_type=MESH)
        pl.semaphore_signal(barrier, inc=1, device_id=(r, row_chip(row_off) * 2 + co), device_id_type=MESH)
    pl.semaphore_signal(barrier, inc=1, device_id=other, device_id_type=MESH)

    for load in loads:
        load.start()

    for load in loads[:4] + loads[5:]:
        load.wait()
    live = tlive[0]
    for store in (gown, hrecv):
        store[NT] = jnp.zeros((HALF, D), BF16)
    gright[NT] = jnp.zeros((2, HALF, D), BF16)
    for store in (gbias, cbias, hbrecv):
        store[NT] = jnp.zeros((1, D), F32)
    bvals[...] = jnp.concatenate([bhalf[...], bhalf[...]], axis=1)
    bacc[...] = jnp.concatenate([bsqhalf[...], bsqhalf[...]], axis=1)
    low = lax.broadcasted_iota(jnp.int32, (1, D), 1) < HALF
    first_row = lax.broadcasted_iota(jnp.int32, (16, D), 0)
    one_rows = jnp.ones((16, D), BF16)

    pl.semaphore_wait(barrier, 2 * NEAR + 1)

    ids = remote(trow_hbm, orow_in, id_ss, id_rs, other)
    for step in range(STEPS):
        half = vals[...].astype(BF16)
        msg[step] = half
        bhalf_now = bvals[...].astype(BF16).astype(F32)
        bmsg[step] = bhalf_now
        for row_off, col_off in zip(ROW_OFF, COL_OFF):
            to = (col_rank(col_off), c)
            remote(msg.at[step], colbuf.at[step, r], ag_ss.at[step, 3], ag_rs.at[step, 3], to).start()
            remote(bmsg.at[step], colb.at[step, r], ag_ss.at[step, 1], ag_rs.at[step, 1], to).start()
            to = (r, row_chip(row_off) * 2 + co)
            remote(msg.at[step], rowbuf.at[step, chip], ag_ss.at[step, 2], ag_rs.at[step, 2], to).start()
            remote(bmsg.at[step], rowb.at[step, chip], ag_ss.at[step, 0], ag_rs.at[step, 0], to).start()
        rowbuf[step, chip] = half
        colbuf[step, r] = half
        rowb[step, chip] = bhalf_now
        colb[step, r] = bhalf_now

        if step == 0:
            ids.start()
            loads[4].wait()
            for s in range(NT):
                for h in range(2):
                    start = pl.multiple_of((co if h == 0 else 1 - co) * HALF, HALF)
                    amounts = cnt[s, pl.ds(start, HALF), :].astype(F32)
                    share = amounts / count_cap
                    root = jnp.sqrt(share)
                    w = jnp.minimum(1.0, root * jnp.sqrt(root))
                    weight[s, h * HALF:(h + 1) * HALF] = jnp.where(s < live, w, 0.0)
                    target[s, h * HALF:(h + 1) * HALF] = jnp.log(jnp.maximum(amounts, 1.0))
            ids.wait_recv()
            fetch = pltpu.make_async_copy(orow_in, orow, in_sem.at[7])
            fetch.start()
            fetch.wait()

        wait_bytes(rowb.at[step, pl.ds(0, NEAR)], ag_rs.at[step, 0])
        wait_bytes(rowbuf.at[step, pl.ds(0, NEAR)], ag_rs.at[step, 2])
        for s in range(NT):
            xsend[step, s] = rowbuf[step, orow[s]]
            xbsend[step, s] = rowb[step, orow[s]]
        cross = remote(xsend.at[step], xrecv.at[step], x_ss.at[step, 0], x_rs.at[step, 0], other)
        bcross = remote(xbsend.at[step], xbrecv.at[step], x_ss.at[step, 1], x_rs.at[step, 1], other)
        cross.start()
        bcross.start()
        wait_bytes(colb.at[step, pl.ds(0, NEAR)], ag_rs.at[step, 1])
        wait_bytes(colbuf.at[step, pl.ds(0, NEAR)], ag_rs.at[step, 3])
        cross.wait_recv()
        bcross.wait_recv()

        e_is, resids, lefts = [], [], []
        for s in range(NT):
            ti, tj = trow[s], tcol[s]
            e_i = jnp.concatenate([rowbuf[step, ti], xrecv[step, s]], axis=0)
            e_j = colbuf[step, pl.ds(2 * tj, 2)].reshape(TILE, D)
            b_i = jnp.where(low, rowb[step, ti], xbrecv[step, s])
            b_j = jnp.where(low, colb[step, 2 * tj], colb[step, 2 * tj + 1])
            lhs = jnp.where(first_row == 0, b_i, jnp.where(first_row == 1, 1.0, 0.0)).astype(BF16)
            rhs = jnp.where(first_row == 0, 1.0, jnp.where(first_row == 1, b_j, 0.0)).astype(BF16)
            score = dot(e_i, e_j, ((1,), (1,))) + dot(lhs, rhs, ((0,), (0,)))
            resid = (weight[s] * (score - target[s])).astype(BF16)
            e_is.append(e_i)
            resids.append(resid)
            lefts.append((dot(resid, e_j, ((1,), (0,))), dot(one_rows, resid, ((1,), (1,)))[0:1]))

        def merged(terms, ids):
            for s in range(NT):
                total, btotal = terms[s]
                for o in range(NT):
                    if o != s:
                        same = jnp.where(ids[o] == ids[s], 1.0, 0.0)
                        total = total + same * terms[o][0]
                        btotal = btotal + same * terms[o][1]
                yield s, total.astype(BF16), btotal

        for s, total, btotal in merged(lefts, trow):
            gown[s] = total[0:HALF]
            goth[step, s] = total[HALF:TILE]
            gbias[s] = btotal
        hcross = remote(goth.at[step], hrecv.at[pl.ds(0, NT)], x_ss.at[step, 2], x_rs.at[step, 2], other)
        hbcross = remote(gbias.at[pl.ds(0, NT)], hbrecv.at[pl.ds(0, NT)], x_ss.at[step, 3], x_rs.at[step, 3], other)
        hcross.start()
        hbcross.start()

        rights = [
            (dot(resids[s], e_is[s], ((0,), (0,))), dot(one_rows, resids[s], ((1,), (0,)))[0:1]) for s in range(NT)
        ]
        for s, total, btotal in merged(rights, tcol):
            gright[s] = total.reshape(2, HALF, D)
            cbias[s] = btotal

        def slot_of(ids, tile):
            found = jnp.int32(NT)
            for s in range(NT):
                found = jnp.where(ids[s] == tile, s, found)
            return found

        for t in range(COL_TILES):
            slot = slot_of(tcol, t)
            csend[step, 2 * t:2 * t + 2] = gright[slot]
            cbsend[step, 2 * t] = cbias[slot]
            cbsend[step, 2 * t + 1] = cbias[slot]
        for k, off in enumerate(COL_OFF):
            to = col_rank(off)
            remote(csend.at[step, to], crecv.at[step, k], rs_ss.at[step, 1],
                   rs_rs.at[step, 1, k // PER], (to, c)).start()
            remote(cbsend.at[step, to], cbrecv.at[step, k], rsb_ss.at[step, 1], rsb_rs.at[step, 1], (to, c)).start()

        hcross.wait_recv()
        hbcross.wait_recv()
        for t in range(ROW_TILES):
            mine, its = slot_of(trow, t), slot_of(orow, t)
            rsend[step, t] = gown[mine] + hrecv[its]
            rbsend[step, t] = gbias[mine] + pltpu.roll(hbrecv[its], HALF, 1)
        for k, off in enumerate(ROW_OFF):
            to = row_chip(off)
            device = (r, to * 2 + co)
            remote(rsend.at[step, to], rrecv.at[step, k], rs_ss.at[step, 0],
                   rs_rs.at[step, 0, k // PER], device).start()
            remote(rbsend.at[step, to], rbrecv.at[step, k], rsb_ss.at[step, 0], rsb_rs.at[step, 0], device).start()

        g = rsend[step, chip].astype(F32) + csend[step, r].astype(F32)
        for half_id, store in ((1, crecv), (0, rrecv)):
            for group in range(GROUPS):
                wait_bytes(store.at[step, pl.ds(group * PER, PER)], rs_rs.at[step, half_id, group])
                for k in range(group * PER, (group + 1) * PER):
                    g = g + store[step, k].astype(F32)

        wait_bytes(cbrecv.at[step], rsb_rs.at[step, 1])
        wait_bytes(rbrecv.at[step], rsb_rs.at[step, 0])
        row_b, col_b = rbsend[step, chip], cbsend[step, r]
        for k in range(NEAR):
            row_b = row_b + rbrecv[step, k]
            col_b = col_b + cbrecv[step, k]

        new_acc = acc[...] + g * g
        new_vals = vals[...] - learn_rate * g / jnp.sqrt(new_acc)
        lane_half = lax.broadcasted_iota(jnp.int32, (1, D), 1) // HALF
        row_b = jnp.where(low, row_b, 0.0)
        col_b = jnp.where(lane_half == z % 2, col_b, 0.0)
        both = row_b + col_b
        bg = both + pltpu.roll(both, HALF, 1)
        new_bacc = bacc[...] + bg * bg
        new_bvals = bvals[...] - learn_rate * bg / jnp.sqrt(new_bacc)
        if step + 1 < STEPS:
            vals[...] = new_vals
            acc[...] = new_acc
            bvals[...] = new_bvals
            bacc[...] = new_bacc
        else:
            emb_out[...] = new_vals
            bias_out[...] = new_bvals[:, 0:HALF]

        if step == 0:
            ids.wait_send()
        for sem, ref in (
            (ag_ss.at[step, 0], rbrecv), (ag_ss.at[step, 1], rbrecv),
            (ag_ss.at[step, 2], rrecv), (ag_ss.at[step, 3], rrecv),
            (rs_ss.at[step, 0], rrecv), (rs_ss.at[step, 1], rrecv),
            (rsb_ss.at[step, 0], rbrecv), (rsb_ss.at[step, 1], rbrecv),
        ):
            wait_bytes(ref.at[step], sem)
        for copy in (cross, bcross, hcross, hbcross):
            copy.wait_send()


def per_device(emb, bias, emb_sq, bias_sq, tile_rows, tile_cols, tile_live, counts):
    hbm = pl.BlockSpec(memory_space=pltpu.HBM)
    vmem = pl.BlockSpec(memory_space=pltpu.VMEM)
    emb_out, bias_out = pl.pallas_call(
        body,
        out_shape=(jax.ShapeDtypeStruct((HALF, D), F32), jax.ShapeDtypeStruct((1, HALF), F32)),
        in_specs=[hbm] * 7 + [pl.BlockSpec(memory_space=pltpu.SMEM)],
        out_specs=(vmem, vmem),
        scratch_shapes=[
            pltpu.VMEM((HALF, D), F32),
            pltpu.VMEM((1, HALF), F32),
            pltpu.VMEM((HALF, D), F32),
            pltpu.VMEM((1, HALF), F32),
            pltpu.VMEM((1, D), F32),
            pltpu.VMEM((1, D), F32),
            pltpu.VMEM((NT, TILE, TILE), jnp.int32),
            pltpu.VMEM((NT, TILE, TILE), F32),
            pltpu.VMEM((NT, TILE, TILE), F32),
            pltpu.SMEM((NT,), jnp.int32),
            pltpu.SMEM((NT,), jnp.int32),
            pltpu.VMEM((NT,), jnp.int32),
            pltpu.SMEM((NT,), jnp.int32),
            pltpu.VMEM((STEPS, HALF, D), BF16),
            pltpu.VMEM((STEPS, 1, D), F32),
            pltpu.VMEM((STEPS, ROW_TILES, HALF, D), BF16),
            pltpu.VMEM((STEPS, ROW_TILES, 1, D), F32),
            pltpu.VMEM((STEPS, 2 * COL_TILES, HALF, D), BF16),
            pltpu.VMEM((STEPS, 2 * COL_TILES, 1, D), F32),
            pltpu.VMEM((STEPS, NT, HALF, D), BF16),
            pltpu.VMEM((STEPS, NT, 1, D), F32),
            pltpu.VMEM((STEPS, NT, HALF, D), BF16),
            pltpu.VMEM((STEPS, NT, 1, D), F32),
            pltpu.VMEM((NT + 1, HALF, D), BF16),
            pltpu.VMEM((STEPS, NT, HALF, D), BF16),
            pltpu.VMEM((NT + 1, 1, D), F32),
            pltpu.VMEM((NT + 1, 2, HALF, D), BF16),
            pltpu.VMEM((NT + 1, 1, D), F32),
            pltpu.VMEM((NT + 1, HALF, D), BF16),
            pltpu.VMEM((NT + 1, 1, D), F32),
            pltpu.VMEM((STEPS, ROW_TILES, HALF, D), BF16),
            pltpu.VMEM((STEPS, ROW_TILES, 1, D), F32),
            pltpu.VMEM((STEPS, NEAR, HALF, D), BF16),
            pltpu.VMEM((STEPS, NEAR, 1, D), F32),
            pltpu.VMEM((STEPS, 2 * COL_TILES, HALF, D), BF16),
            pltpu.VMEM((STEPS, 2 * COL_TILES, 1, D), F32),
            pltpu.VMEM((STEPS, NEAR, HALF, D), BF16),
            pltpu.VMEM((STEPS, NEAR, 1, D), F32),
            pltpu.SemaphoreType.DMA((8,)),
            pltpu.SemaphoreType.DMA,
            pltpu.SemaphoreType.DMA,
            pltpu.SemaphoreType.DMA((STEPS, 4)),
            pltpu.SemaphoreType.DMA((STEPS, 4)),
            pltpu.SemaphoreType.DMA((STEPS, 4)),
            pltpu.SemaphoreType.DMA((STEPS, 4)),
            pltpu.SemaphoreType.DMA((STEPS, 2)),
            pltpu.SemaphoreType.DMA((STEPS, 2, GROUPS)),
            pltpu.SemaphoreType.DMA((STEPS, 2)),
            pltpu.SemaphoreType.DMA((STEPS, 2)),
        ],
        compiler_params=pltpu.CompilerParams(
            collective_id=0, has_side_effects=True, vmem_limit_bytes=40 * 1024 * 1024
        ),
    )(
        *(
            pltpu.with_memory_space_constraint(v, pltpu.HBM)
            for v in (
                emb, bias.reshape(1, HALF), emb_sq, bias_sq.reshape(1, HALF), counts,
                tile_rows, tile_cols,
            )
        ),
        tile_live,
    )
    return (emb_out, bias_out.reshape(HALF))


def solution(mesh):
    placed = (
        P(("row", "col"), None),
        P(("row", "col")),
        P(("row", "col"), None),
        P(("row", "col")),
        P(("row", "col")),
        P(("row", "col")),
        P(("row", "col")),
        P(("row", "col"), None, None),
    )
    return jax.shard_map(
        per_device,
        mesh=mesh,
        in_specs=placed,
        out_specs=(P(("row", "col"), None), P(("row", "col"))),
        check_vma=False,
    )
```

```python
import jax
import jax.numpy as jnp
from jax import lax
from jax.experimental import pallas as pl
from jax.experimental.pallas import tpu as pltpu
from jax.sharding import PartitionSpec as P

MESH = pl.DeviceIdType.MESH
D = 128
TILE = 128
HALF = 64
NT = 4
STEPS = 2
ROW_TILES = 16
COL_TILES = 8
NEAR = 15
GROUPS = 3
PER = NEAR // GROUPS
WHOLE = [(0, HALF)]
SPLIT = [(0, HALF // 2), (HALF // 2, HALF // 2)]
GATHER_PARTS = [WHOLE] + [SPLIT] * (STEPS - 1)
RETURN_PARTS = [SPLIT] * (STEPS - 1) + [WHOLE]

learn_rate = 0.1
count_cap = 100.0

F32 = jnp.float32
BF16 = jnp.bfloat16

OFFSETS = [(a, b) for a in range(8) for b in range(2) if a or b]
ROW_OFF = sorted(OFFSETS, key=lambda o: -(min(o[0], 8 - o[0]) + o[1]))
COL_OFF = sorted(OFFSETS, key=lambda o: -(min(o[0], 8 - o[0]) + 2 * o[1]))


def dot(a, b, dims):
    return lax.dot_general(a, b, (dims, ((), ())), preferred_element_type=F32)


def body(
    emb_hbm, bias_hbm, esq_hbm, bsq_hbm, counts_hbm, trow_hbm, tcol_hbm, tlive,
    out,
    vals, bhalf, acc, bsqhalf, bvals, bacc, cnt, weight, target,
    trow, tcol, orow_in, orow,
    msg, bmsg, rowbuf, rowb, colbuf, colb, xsend, xbsend, xrecv, xbrecv,
    gown, goth, gbias, gright, cbias, hrecv, hbrecv,
    rsend, rbsend, rrecv, rbrecv, csend, cbsend, crecv, cbrecv,
    in_sem, id_ss, id_rs, ag_ss, ag_rs, x_ss, x_rs, rs_ss, rs_rs, rsb_ss, rsb_rs,
):
    r, c = lax.axis_index("row"), lax.axis_index("col")
    xh, z = r // 8, r % 8
    y, xl, co = c // 4, (c // 2) % 2, c % 2
    chip = c // 2

    def row_chip(off):
        return ((y + off[0]) % 8) * 2 + (xl + off[1]) % 2

    def col_rank(off):
        return ((xh + off[1]) % 2) * 8 + (z + off[0]) % 8

    other = (r, chip * 2 + 1 - co)

    def remote(src, dst, ss, rs, device):
        return pltpu.make_async_remote_copy(
            src_ref=src, dst_ref=dst, send_sem=ss, recv_sem=rs, device_id=device, device_id_type=MESH
        )

    def wait_bytes(ref, sem):
        pltpu.make_async_copy(ref, ref, sem).wait()

    loads = [
        pltpu.make_async_copy(src, dst, in_sem.at[i])
        for i, (src, dst) in enumerate(
            (
                (emb_hbm, vals), (bias_hbm, bhalf), (esq_hbm, acc), (bsq_hbm, bsqhalf),
                (counts_hbm, cnt), (trow_hbm, trow), (tcol_hbm, tcol),
            )
        )
    ]
    barrier = pltpu.get_barrier_semaphore()
    for row_off, col_off in zip(ROW_OFF, COL_OFF):
        pl.semaphore_signal(barrier, inc=1, device_id=(col_rank(col_off), c), device_id_type=MESH)
        pl.semaphore_signal(barrier, inc=1, device_id=(r, row_chip(row_off) * 2 + co), device_id_type=MESH)
    pl.semaphore_signal(barrier, inc=1, device_id=other, device_id_type=MESH)

    for load in loads:
        load.start()

    for load in loads[:4] + loads[5:]:
        load.wait()
    live = tlive[0]
    for store in (gown, hrecv):
        store[NT] = jnp.zeros((HALF, D), BF16)
    gright[NT] = jnp.zeros((2, HALF, D), BF16)
    for store in (gbias, cbias, hbrecv):
        store[NT] = jnp.zeros((1, D), F32)
    bvals[...] = jnp.concatenate([bhalf[...], bhalf[...]], axis=1)
    bacc[...] = jnp.concatenate([bsqhalf[...], bsqhalf[...]], axis=1)
    low = lax.broadcasted_iota(jnp.int32, (1, D), 1) < HALF
    first_row = lax.broadcasted_iota(jnp.int32, (16, D), 0)
    one_rows = jnp.ones((16, D), BF16)

    pl.semaphore_wait(barrier, 2 * NEAR + 1)

    ids = remote(trow_hbm, orow_in, id_ss, id_rs, other)
    def send_gather(step, part, with_bias):
        lo, n = GATHER_PARTS[step][part]
        rows = pl.ds(lo, n)
        half = vals[lo:lo + n].astype(BF16)
        msg[step, lo:lo + n] = half
        if with_bias:
            bhalf_now = bvals[...].astype(BF16).astype(F32)
            bmsg[step] = bhalf_now
        for row_off, col_off in zip(ROW_OFF, COL_OFF):
            to = (col_rank(col_off), c)
            remote(msg.at[step, rows], colbuf.at[step, r, rows], ag_ss.at[step, 3], ag_rs.at[step, 3, part], to).start()
            if with_bias:
                remote(bmsg.at[step], colb.at[step, r], ag_ss.at[step, 1], ag_rs.at[step, 1, 0], to).start()
            to = (r, row_chip(row_off) * 2 + co)
            remote(msg.at[step, rows], rowbuf.at[step, chip, rows], ag_ss.at[step, 2], ag_rs.at[step, 2, part], to).start()
            if with_bias:
                remote(bmsg.at[step], rowb.at[step, chip], ag_ss.at[step, 0], ag_rs.at[step, 0, 0], to).start()
        rowbuf[step, chip, lo:lo + n] = half
        colbuf[step, r, lo:lo + n] = half
        if with_bias:
            rowb[step, chip] = bhalf_now
            colb[step, r] = bhalf_now

    send_gather(0, 0, True)
    for step in range(STEPS):
        if step == 0:
            ids.start()
            loads[4].wait()
            for s in range(NT):
                for h in range(2):
                    start = pl.multiple_of((co if h == 0 else 1 - co) * HALF, HALF)
                    amounts = cnt[s, pl.ds(start, HALF), :].astype(F32)
                    share = amounts / count_cap
                    root = jnp.sqrt(share)
                    w = jnp.minimum(1.0, root * jnp.sqrt(root))
                    weight[s, h * HALF:(h + 1) * HALF] = jnp.where(s < live, w, 0.0)
                    target[s, h * HALF:(h + 1) * HALF] = jnp.log(jnp.maximum(amounts, 1.0))
            ids.wait_recv()
            fetch = pltpu.make_async_copy(orow_in, orow, in_sem.at[7])
            fetch.start()
            fetch.wait()

        for part, (lo, n) in enumerate(GATHER_PARTS[step]):
            wait_bytes(rowbuf.at[step, pl.ds(0, NEAR), pl.ds(lo, n)], ag_rs.at[step, 2, part])
        wait_bytes(rowb.at[step, pl.ds(0, NEAR)], ag_rs.at[step, 0, 0])
        for s in range(NT):
            xsend[step, s] = rowbuf[step, orow[s]]
            xbsend[step, s] = rowb[step, orow[s]]
        cross = remote(xsend.at[step], xrecv.at[step], x_ss.at[step, 0], x_rs.at[step, 0], other)
        bcross = remote(xbsend.at[step], xbrecv.at[step], x_ss.at[step, 1], x_rs.at[step, 1], other)
        cross.start()
        bcross.start()
        for part, (lo, n) in enumerate(GATHER_PARTS[step]):
            wait_bytes(colbuf.at[step, pl.ds(0, NEAR), pl.ds(lo, n)], ag_rs.at[step, 3, part])
        wait_bytes(colb.at[step, pl.ds(0, NEAR)], ag_rs.at[step, 1, 0])
        cross.wait_recv()
        bcross.wait_recv()

        e_is, resids, lefts = [], [], []
        for s in range(NT):
            ti, tj = trow[s], tcol[s]
            e_i = jnp.concatenate([rowbuf[step, ti], xrecv[step, s]], axis=0)
            e_j = colbuf[step, pl.ds(2 * tj, 2)].reshape(TILE, D)
            b_i = jnp.where(low, rowb[step, ti], xbrecv[step, s])
            b_j = jnp.where(low, colb[step, 2 * tj], colb[step, 2 * tj + 1])
            lhs = jnp.where(first_row == 0, b_i, jnp.where(first_row == 1, 1.0, 0.0)).astype(BF16)
            rhs = jnp.where(first_row == 0, 1.0, jnp.where(first_row == 1, b_j, 0.0)).astype(BF16)
            score = dot(e_i, e_j, ((1,), (1,))) + dot(lhs, rhs, ((0,), (0,)))
            resid = (weight[s] * (score - target[s])).astype(BF16)
            e_is.append(e_i)
            resids.append(resid)
            lefts.append((dot(resid, e_j, ((1,), (0,))), dot(one_rows, resid, ((1,), (1,)))[0:1]))

        def merged(terms, ids):
            for s in range(NT):
                total, btotal = terms[s]
                for o in range(NT):
                    if o != s:
                        same = jnp.where(ids[o] == ids[s], 1.0, 0.0)
                        total = total + same * terms[o][0]
                        btotal = btotal + same * terms[o][1]
                yield s, total.astype(BF16), btotal

        for s, total, btotal in merged(lefts, trow):
            gown[s] = total[0:HALF]
            goth[step, s] = total[HALF:TILE]
            gbias[s] = btotal
        hcross = remote(goth.at[step], hrecv.at[pl.ds(0, NT)], x_ss.at[step, 2], x_rs.at[step, 2], other)
        hbcross = remote(gbias.at[pl.ds(0, NT)], hbrecv.at[pl.ds(0, NT)], x_ss.at[step, 3], x_rs.at[step, 3], other)
        hcross.start()
        hbcross.start()

        rights = [
            (dot(resids[s], e_is[s], ((0,), (0,))), dot(one_rows, resids[s], ((1,), (0,)))[0:1]) for s in range(NT)
        ]
        for s, total, btotal in merged(rights, tcol):
            gright[s] = total.reshape(2, HALF, D)
            cbias[s] = btotal

        def slot_of(ids, tile):
            found = jnp.int32(NT)
            for s in range(NT):
                found = jnp.where(ids[s] == tile, s, found)
            return found

        for t in range(COL_TILES):
            slot = slot_of(tcol, t)
            csend[step, 2 * t:2 * t + 2] = gright[slot]
            cbsend[step, 2 * t] = cbias[slot]
            cbsend[step, 2 * t + 1] = cbias[slot]
        parts = RETURN_PARTS[step]

        def send_columns(part):
            lo, n = parts[part]
            for k, off in enumerate(COL_OFF):
                to = col_rank(off)
                sem = rs_rs.at[step, 1, part if len(parts) > 1 else k // PER]
                remote(csend.at[step, to, pl.ds(lo, n)], crecv.at[step, k, pl.ds(lo, n)],
                       rs_ss.at[step, 1], sem, (to, c)).start()
                if part == 0:
                    remote(cbsend.at[step, to], cbrecv.at[step, k],
                           rsb_ss.at[step, 1], rsb_rs.at[step, 1], (to, c)).start()

        def send_rows(part):
            lo, n = parts[part]
            for k, off in enumerate(ROW_OFF):
                to = row_chip(off)
                device = (r, to * 2 + co)
                sem = rs_rs.at[step, 0, part if len(parts) > 1 else k // PER]
                remote(rsend.at[step, to, pl.ds(lo, n)], rrecv.at[step, k, pl.ds(lo, n)],
                       rs_ss.at[step, 0], sem, device).start()
                if part == 0:
                    remote(rbsend.at[step, to], rbrecv.at[step, k],
                           rsb_ss.at[step, 0], rsb_rs.at[step, 0], device).start()

        send_columns(0)

        hcross.wait_recv()
        hbcross.wait_recv()
        for t in range(ROW_TILES):
            mine, its = slot_of(trow, t), slot_of(orow, t)
            rsend[step, t] = gown[mine] + hrecv[its]
            rbsend[step, t] = gbias[mine] + pltpu.roll(hbrecv[its], HALF, 1)
        send_rows(0)
        for part in range(1, len(parts)):
            send_columns(part)
            send_rows(part)

        last = step + 1 == STEPS
        for part, (lo, n) in enumerate(parts):
            g = rsend[step, chip, lo:lo + n].astype(F32) + csend[step, r, lo:lo + n].astype(F32)
            for side, store in ((1, crecv), (0, rrecv)):
                if len(parts) > 1:
                    wait_bytes(store.at[step, pl.ds(0, NEAR), pl.ds(lo, n)], rs_rs.at[step, side, part])
                for k in range(NEAR):
                    if len(parts) == 1 and k % PER == 0:
                        wait_bytes(store.at[step, pl.ds(k, PER)], rs_rs.at[step, side, k // PER])
                    g = g + store[step, k, lo:lo + n].astype(F32)
            new_acc = acc[lo:lo + n] + g * g
            new_vals = vals[lo:lo + n] - learn_rate * g / jnp.sqrt(new_acc)
            if last:
                out[lo:lo + n] = new_vals
            else:
                vals[lo:lo + n] = new_vals
                acc[lo:lo + n] = new_acc
            if part + 1 < len(parts):
                if not last:
                    send_gather(step + 1, part, False)
                continue

            wait_bytes(cbrecv.at[step], rsb_rs.at[step, 1])
            wait_bytes(rbrecv.at[step], rsb_rs.at[step, 0])
            row_b, col_b = rbsend[step, chip], cbsend[step, r]
            for k in range(NEAR):
                row_b = row_b + rbrecv[step, k]
                col_b = col_b + cbrecv[step, k]
            lane_half = lax.broadcasted_iota(jnp.int32, (1, D), 1) // HALF
            both = jnp.where(low, row_b, 0.0) + jnp.where(lane_half == z % 2, col_b, 0.0)
            bg = both + pltpu.roll(both, HALF, 1)
            new_bacc = bacc[...] + bg * bg
            new_bvals = bvals[...] - learn_rate * bg / jnp.sqrt(new_bacc)
            if last:
                out[HALF:HALF + 8] = jnp.broadcast_to(new_bvals, (8, D))
            else:
                bvals[...] = new_bvals
                bacc[...] = new_bacc
                send_gather(step + 1, part, True)

        if step == 0:
            ids.wait_send()
        for sem, ref in (
            (ag_ss.at[step, 0], rbrecv), (ag_ss.at[step, 1], rbrecv),
            (ag_ss.at[step, 2], rrecv), (ag_ss.at[step, 3], rrecv),
            (rs_ss.at[step, 0], rrecv), (rs_ss.at[step, 1], rrecv),
            (rsb_ss.at[step, 0], rbrecv), (rsb_ss.at[step, 1], rbrecv),
        ):
            wait_bytes(ref.at[step], sem)
        for copy in (cross, bcross, hcross, hbcross):
            copy.wait_send()


def per_device(emb, bias, emb_sq, bias_sq, tile_rows, tile_cols, tile_live, counts):
    hbm = pl.BlockSpec(memory_space=pltpu.HBM)
    vmem = pl.BlockSpec(memory_space=pltpu.VMEM)
    out = pl.pallas_call(
        body,
        out_shape=jax.ShapeDtypeStruct((HALF + 8, D), F32),
        in_specs=[hbm] * 7 + [pl.BlockSpec(memory_space=pltpu.SMEM)],
        out_specs=vmem,
        scratch_shapes=[
            pltpu.VMEM((HALF, D), F32),
            pltpu.VMEM((1, HALF), F32),
            pltpu.VMEM((HALF, D), F32),
            pltpu.VMEM((1, HALF), F32),
            pltpu.VMEM((1, D), F32),
            pltpu.VMEM((1, D), F32),
            pltpu.VMEM((NT, TILE, TILE), jnp.int32),
            pltpu.VMEM((NT, TILE, TILE), F32),
            pltpu.VMEM((NT, TILE, TILE), F32),
            pltpu.SMEM((NT,), jnp.int32),
            pltpu.SMEM((NT,), jnp.int32),
            pltpu.VMEM((NT,), jnp.int32),
            pltpu.SMEM((NT,), jnp.int32),
            pltpu.VMEM((STEPS, HALF, D), BF16),
            pltpu.VMEM((STEPS, 1, D), F32),
            pltpu.VMEM((STEPS, ROW_TILES, HALF, D), BF16),
            pltpu.VMEM((STEPS, ROW_TILES, 1, D), F32),
            pltpu.VMEM((STEPS, 2 * COL_TILES, HALF, D), BF16),
            pltpu.VMEM((STEPS, 2 * COL_TILES, 1, D), F32),
            pltpu.VMEM((STEPS, NT, HALF, D), BF16),
            pltpu.VMEM((STEPS, NT, 1, D), F32),
            pltpu.VMEM((STEPS, NT, HALF, D), BF16),
            pltpu.VMEM((STEPS, NT, 1, D), F32),
            pltpu.VMEM((NT + 1, HALF, D), BF16),
            pltpu.VMEM((STEPS, NT, HALF, D), BF16),
            pltpu.VMEM((NT + 1, 1, D), F32),
            pltpu.VMEM((NT + 1, 2, HALF, D), BF16),
            pltpu.VMEM((NT + 1, 1, D), F32),
            pltpu.VMEM((NT + 1, HALF, D), BF16),
            pltpu.VMEM((NT + 1, 1, D), F32),
            pltpu.VMEM((STEPS, ROW_TILES, HALF, D), BF16),
            pltpu.VMEM((STEPS, ROW_TILES, 1, D), F32),
            pltpu.VMEM((STEPS, NEAR, HALF, D), BF16),
            pltpu.VMEM((STEPS, NEAR, 1, D), F32),
            pltpu.VMEM((STEPS, 2 * COL_TILES, HALF, D), BF16),
            pltpu.VMEM((STEPS, 2 * COL_TILES, 1, D), F32),
            pltpu.VMEM((STEPS, NEAR, HALF, D), BF16),
            pltpu.VMEM((STEPS, NEAR, 1, D), F32),
            pltpu.SemaphoreType.DMA((8,)),
            pltpu.SemaphoreType.DMA,
            pltpu.SemaphoreType.DMA,
            pltpu.SemaphoreType.DMA((STEPS, 4)),
            pltpu.SemaphoreType.DMA((STEPS, 4, 2)),
            pltpu.SemaphoreType.DMA((STEPS, 4)),
            pltpu.SemaphoreType.DMA((STEPS, 4)),
            pltpu.SemaphoreType.DMA((STEPS, 2)),
            pltpu.SemaphoreType.DMA((STEPS, 2, GROUPS)),
            pltpu.SemaphoreType.DMA((STEPS, 2)),
            pltpu.SemaphoreType.DMA((STEPS, 2)),
        ],
        compiler_params=pltpu.CompilerParams(
            collective_id=0, has_side_effects=True, vmem_limit_bytes=40 * 1024 * 1024
        ),
    )(
        *(
            pltpu.with_memory_space_constraint(v, pltpu.HBM)
            for v in (
                emb, bias.reshape(1, HALF), emb_sq, bias_sq.reshape(1, HALF), counts,
                tile_rows, tile_cols,
            )
        ),
        tile_live,
    )
    return (out[:HALF], out[HALF, :HALF])


def solution(mesh):
    placed = (
        P(("row", "col"), None),
        P(("row", "col")),
        P(("row", "col"), None),
        P(("row", "col")),
        P(("row", "col")),
        P(("row", "col")),
        P(("row", "col")),
        P(("row", "col"), None, None),
    )
    return jax.shard_map(
        per_device,
        mesh=mesh,
        in_specs=placed,
        out_specs=(P(("row", "col"), None), P(("row", "col"))),
        check_vma=False,
    )
```
